32 devices in a mesh: row: 8 (over z, x), col: 4 (over y, core).
Axes of the slice: x: 2, y: 2, z: 4, core: 2. Of those that a mesh axis runs over, the one named last changes fastest.
Arguments:
- field: bfloat16 [1, 64, 512, 512], P(None, None, 'row', 'col'), may hold values from -6 to 6
- x_weight: float32 [2, 2, 12, 64, 64], replicated, may hold values from -2 to 2
- y_weight: float32 [2, 2, 12, 64, 64], replicated, may hold values from -2 to 2
- up_weight: bfloat16 [2, 256, 64], replicated, may hold values from -0.75 to 0.75
- up_bias: float32 [2, 256], replicated, may hold values from -3 to 3
- down_weight: bfloat16 [2, 64, 256], replicated, may hold values from -0.375 to 0.375
Outputs:
- result: bfloat16 [1, 64, 512, 512], P(None, None, 'row', 'col')
The draws below stay inside these ranges and needn't reach their ends.
All inputs are finite; a program needn't handle non-finite values.
Results may differ from the reference program's by a relative error of at most 0.025.
Values may be sent and summed in bfloat16 or wider, within the bound.
A program may use at most 64 MiB of HBM per device.

```python
import math
import jax
import jax.numpy as jnp
from jax import lax

C = 64
H = 256
MODES = 12
LAYERS = 2
Z = 1
NX = 512
NY = 512


def steps_of(own_key, dims, split, smallest, largest):
    loudness = 1.0
    for axis_at, shards_of in split:
        heights = jax.random.uniform(jax.random.fold_in(jax.random.fold_in(own_key, 6), axis_at), (shards_of,), jnp.float32, smallest / len(split), largest / len(split))
        loudness = loudness * jnp.repeat(jnp.exp(heights), dims[axis_at] // shards_of).reshape((-1,) + (1,) * (len(dims) - 1 - axis_at))
    return loudness


def normal_values(stream_key, extent, deviation, bound, split=(), kind=jnp.bfloat16):
    result = jax.random.normal(stream_key, extent, jnp.float32) * deviation
    if len(split) > 0:
        result = steps_of(stream_key, extent, split, -0.22, 0.18) * result
    return jnp.clip(result, min=-bound, max=bound).astype(kind)


def setup_inputs(seed: int = 0) -> dict:
    key_list = jax.random.split(jax.random.key(seed), 7)
    field = normal_values(key_list[0], (Z, C, NX, NY), 1.0, 6.0, ((2, 8), (3, 4)))
    x_weight = normal_values(key_list[1], (LAYERS, 2, MODES, C, C), 0.35, 2.0, (), jnp.float32)
    y_weight = normal_values(key_list[2], (LAYERS, 2, MODES, C, C), 0.35, 2.0, (), jnp.float32)
    up_weight = normal_values(key_list[3], (LAYERS, H, C), C ** -0.5, 0.75)
    up_bias = normal_values(key_list[4], (LAYERS, H), 0.5, 3.0, (), jnp.float32)
    down_weight = normal_values(key_list[5], (LAYERS, C, H), H ** -0.5, 0.375)
    return {"field": field, "x_weight": x_weight, "y_weight": y_weight, "up_weight": up_weight, "up_bias": up_bias, "down_weight": down_weight}


def tables(total, count):
    pos = jnp.arange(count, dtype=jnp.int32)
    kays = jnp.arange(MODES, dtype=jnp.int32)
    phase = (kays[:, None] * pos[None, :]) % total
    angle = phase.astype(jnp.float32) * (2.0 * math.pi / total)
    cosine = jnp.cos(angle)
    sine = jnp.sin(angle)
    forward = jnp.concatenate([cosine, -sine], axis=0).astype(jnp.bfloat16)
    factor = (jnp.where(kays == 0, 1.0, 2.0) / total).astype(jnp.float32)[:, None]
    inverse = jnp.concatenate([cosine * factor, -sine * factor], axis=0).astype(jnp.bfloat16)
    return forward, inverse


def mix_modes(modes, weight):
    first = modes[:, :MODES]
    second = modes[:, MODES:]
    hi = lax.Precision.HIGHEST
    real_part = jnp.einsum("kco,zkcr->zkor", weight[0], first, precision=hi) - jnp.einsum("kco,zkcr->zkor", weight[1], second, precision=hi)
    imag_part = jnp.einsum("kco,zkcr->zkor", weight[1], first, precision=hi) + jnp.einsum("kco,zkcr->zkor", weight[0], second, precision=hi)
    return jnp.concatenate([real_part, imag_part], axis=1).astype(jnp.bfloat16)


def feed_block(block, w_up, b_up, w_down):
    hidden = jnp.einsum("hc,zcxy->zhxy", w_up.astype(jnp.float32), block.astype(jnp.float32))
    hidden = jax.nn.gelu(hidden + b_up[None, :, None, None], approximate=False).astype(jnp.bfloat16)
    back = jnp.einsum("ch,zhxy->zcxy", w_down.astype(jnp.float32), hidden.astype(jnp.float32))
    return (block.astype(jnp.float32) + back).astype(jnp.bfloat16)


def reference(field, x_weight, y_weight, up_weight, up_bias, down_weight):
    fwd_x, inv_x = tables(NX, NX)
    fwd_y, inv_y = tables(NY, NY)
    block = 64
    state = field
    for layer in range(LAYERS):
        wide = state.astype(jnp.float32)
        xmodes = jnp.einsum("mx,zcxy->zmcy", fwd_x.astype(jnp.float32), wide)
        xmixed = mix_modes(xmodes, x_weight[layer])
        back_x = jnp.einsum("mx,zmoy->zoxy", inv_x.astype(jnp.float32), xmixed.astype(jnp.float32))
        ymodes = jnp.einsum("my,zcxy->zmcx", fwd_y.astype(jnp.float32), wide)
        ymixed = mix_modes(ymodes, y_weight[layer])
        back_y = jnp.einsum("my,zmox->zoxy", inv_y.astype(jnp.float32), ymixed.astype(jnp.float32))
        gfield = (wide + back_x + back_y).astype(jnp.bfloat16)
        pieces = gfield.reshape(Z, C, NX // block, block, NY).transpose(2, 0, 1, 3, 4)
        w_up = up_weight[layer]
        b_up = up_bias[layer]
        w_down = down_weight[layer]
        done = lax.map(lambda piece: feed_block(piece, w_up, b_up, w_down), pieces)
        state = done.transpose(1, 2, 0, 3, 4).reshape(Z, C, NX, NY)
    return state
```

```python
import functools
import math

import jax
import jax.numpy as jnp
from jax import lax
from jax.experimental import pallas as pl
from jax.experimental.pallas import tpu as pltpu
from jax.sharding import PartitionSpec as P

MODES = 12
LAYERS = 2
MESH = pl.DeviceIdType.MESH
VMEM = pltpu.VMEM


def tables(total, start, count):
    pos = start + jnp.arange(count, dtype=jnp.int32)
    kays = jnp.arange(MODES, dtype=jnp.int32)
    phase = kays[:, None] * pos[None, :] % total
    angle = phase.astype(jnp.float32) * (2.0 * math.pi / total)
    both = jnp.stack([jnp.cos(angle), -jnp.sin(angle)], axis=1)
    factor = (jnp.where(kays == 0, 1.0, 2.0) / total).astype(jnp.float32)[:, None, None]
    forward = both.astype(jnp.bfloat16).reshape(2 * MODES, count)
    inverse = (both * factor).astype(jnp.bfloat16).reshape(2 * MODES, count)
    return forward, inverse


def exchange_kernel(
    nr, nc, x_in, y_in, wx, wy, x_out, y_out, x_got, y_got, x_mat, y_mat,
    xs_send, xs_recv, ys_send, ys_recv, xg_send, xg_recv, yg_send, yg_recv,
):
    row = lax.axis_index("row")
    col = lax.axis_index("col")

    def row_peer(d):
        return (lax.rem(row + d, nr), col)

    def col_peer(d):
        return (row, lax.rem(col + d, nc))

    barrier = pltpu.get_barrier_semaphore()
    for d in range(1, nr):
        pl.semaphore_signal(barrier, inc=1, device_id=row_peer(d), device_id_type=MESH)
    for d in range(1, nc):
        pl.semaphore_signal(barrier, inc=1, device_id=col_peer(d), device_id_type=MESH)
    pl.semaphore_wait(barrier, nr + nc - 2)

    def copy(src, dst, send, recv, d, peer):
        made = pltpu.make_async_remote_copy(
            src_ref=src, dst_ref=dst, send_sem=send.at[d], recv_sem=recv.at[d],
            device_id=peer, device_id_type=MESH,
        )
        made.start()
        return made

    y_scatter = [
        copy(y_in.at[col_peer(d)[1]], y_got.at[d], ys_send, ys_recv, d, col_peer(d))
        for d in range(1, nc)
    ]
    x_scatter = [
        copy(x_in.at[row_peer(d)[0]], x_got.at[d], xs_send, xs_recv, d, row_peer(d))
        for d in range(1, nr)
    ]

    for w, mat in ((wy, y_mat), (wx, x_mat)):
        for k in range(MODES):
            real = w[0, k].astype(jnp.bfloat16)
            imag = w[1, k].astype(jnp.bfloat16)
            top = jnp.concatenate([real, imag], axis=1)
            bottom = jnp.concatenate([-imag, real], axis=1)
            mat[k] = jnp.concatenate([top, bottom], axis=0)

    def mix(own, first, got, n, mat, out):
        width = mat.shape[1]
        for k in range(MODES):
            lanes = pl.ds(k * width, width)
            total = first[own, :, lanes].astype(jnp.float32)
            for d in range(1, n):
                total = total + got[d, :, lanes].astype(jnp.float32)
            out[own, :, lanes] = jnp.dot(
                total.astype(jnp.bfloat16), mat[k], preferred_element_type=jnp.float32
            ).astype(jnp.bfloat16)

    for made in y_scatter:
        made.wait()
    mix(col, y_in, y_got, nc, y_mat, y_out)
    y_gather = [
        copy(y_out.at[col], y_out.at[col], yg_send, yg_recv, d, col_peer(d))
        for d in range(1, nc)
    ]
    for made in x_scatter:
        made.wait()
    mix(row, x_in, x_got, nr, x_mat, x_out)
    x_gather = [
        copy(x_out.at[row], x_out.at[row], xg_send, xg_recv, d, row_peer(d))
        for d in range(1, nr)
    ]
    for made in y_gather + x_gather:
        made.wait()


def exchange(x_part, y_part, wx, wy):
    nr, nc = lax.axis_size("row"), lax.axis_size("col")
    channels = wx.shape[-1]
    wide = 2 * channels
    x_shape = (nr, x_part.shape[0] // nr, MODES * wide)
    y_shape = (nc, y_part.shape[0] // nc, MODES * wide)
    dma = pltpu.SemaphoreType.DMA
    x_all, y_all = pl.pallas_call(
        functools.partial(exchange_kernel, nr, nc),
        out_shape=(
            jax.ShapeDtypeStruct(x_shape, jnp.bfloat16),
            jax.ShapeDtypeStruct(y_shape, jnp.bfloat16),
        ),
        in_specs=[pl.BlockSpec(memory_space=VMEM)] * 4,
        out_specs=(pl.BlockSpec(memory_space=VMEM),) * 2,
        scratch_shapes=[
            VMEM(x_shape, jnp.bfloat16),
            VMEM(y_shape, jnp.bfloat16),
            VMEM((MODES, wide, wide), jnp.bfloat16),
            VMEM((MODES, wide, wide), jnp.bfloat16),
            dma((nr,)), dma((nr,)), dma((nc,)), dma((nc,)),
            dma((nr,)), dma((nr,)), dma((nc,)), dma((nc,)),
        ],
        compiler_params=pltpu.CompilerParams(
            collective_id=0, has_side_effects=True, vmem_limit_bytes=32 << 20
        ),
        name="exchange",
    )(x_part.reshape(x_shape), y_part.reshape(y_shape), wx, wy)
    return (
        x_all.reshape(x_part.shape[0], 2 * MODES, channels),
        y_all.reshape(y_part.shape[0], 2 * MODES, channels),
    )


def feed_kernel(g_ref, up_ref, bias_ref, down_ref, out_ref):
    up = up_ref[...]
    bias = bias_ref[...]
    down = down_ref[...]
    for at in range(g_ref.shape[0]):
        block = g_ref[at]
        hidden = jnp.dot(up, block, preferred_element_type=jnp.float32) + bias
        hidden = (0.5 * hidden * (1.0 + lax.erf(hidden * math.sqrt(0.5)))).astype(jnp.bfloat16)
        back = jnp.dot(down, hidden, preferred_element_type=jnp.float32)
        out_ref[at] = (block.astype(jnp.float32) + back).astype(jnp.bfloat16)


def feed(gfield, up, bias, down):
    lines, channels, cols = gfield.shape
    step = math.gcd(lines, 4)
    units = up.shape[0]
    return pl.pallas_call(
        feed_kernel,
        grid=(lines // step,),
        out_shape=jax.ShapeDtypeStruct(gfield.shape, jnp.bfloat16),
        in_specs=[
            pl.BlockSpec((step, channels, cols), lambda i: (i, 0, 0)),
            pl.BlockSpec((units, channels), lambda i: (0, 0)),
            pl.BlockSpec((units, 1), lambda i: (0, 0)),
            pl.BlockSpec((channels, units), lambda i: (0, 0)),
        ],
        out_specs=pl.BlockSpec((step, channels, cols), lambda i: (i, 0, 0)),
        compiler_params=pltpu.CompilerParams(vmem_limit_bytes=32 << 20),
        name="feed",
    )(gfield, up, bias[:, None], down)


def on_device(field, x_weight, y_weight, up_weight, up_bias, down_weight):
    planes, channels, rows_here, cols_here = field.shape
    total_x = rows_here * lax.axis_size("row")
    total_y = cols_here * lax.axis_size("col")
    fwd_x, inv_x = tables(total_x, lax.axis_index("row") * rows_here, rows_here)
    fwd_y, inv_y = tables(total_y, lax.axis_index("col") * cols_here, cols_here)
    results = []
    for z in range(planes):
        state = field[z].transpose(1, 0, 2)
        for layer in range(LAYERS):
            x_part = jnp.einsum("mx,xcy->ymc", fwd_x, state, preferred_element_type=jnp.float32)
            y_part = jnp.einsum("my,xcy->xmc", fwd_y, state, preferred_element_type=jnp.float32)
            x_mixed, y_mixed = exchange(
                x_part.astype(jnp.bfloat16), y_part.astype(jnp.bfloat16),
                x_weight[layer], y_weight[layer],
            )
            back_x = jnp.einsum("mx,ymo->xoy", inv_x, x_mixed, preferred_element_type=jnp.float32)
            back_y = jnp.einsum("my,xmo->xoy", inv_y, y_mixed, preferred_element_type=jnp.float32)
            gfield = (state.astype(jnp.float32) + back_x + back_y).astype(jnp.bfloat16)
            state = feed(gfield, up_weight[layer], up_bias[layer], down_weight[layer])
        results.append(state.transpose(1, 0, 2))
    return jnp.stack(results)


def solution(mesh):
    in_specs = (P(None, None, "row", "col"), P(), P(), P(), P(), P())
    out_specs = P(None, None, "row", "col")
    return jax.shard_map(
        on_device, mesh=mesh, in_specs=in_specs, out_specs=out_specs, check_vma=False
    )
```

```python
import functools
import math

import jax
import jax.numpy as jnp
from jax import lax
from jax.experimental import pallas as pl
from jax.experimental.pallas import tpu as pltpu
from jax.sharding import PartitionSpec as P

MODES = 12
LAYERS = 2
MESH = pl.DeviceIdType.MESH
VMEM = pltpu.VMEM


def tables(total, start, count):
    pos = start + jnp.arange(count, dtype=jnp.int32)
    kays = jnp.arange(MODES, dtype=jnp.int32)
    phase = kays[:, None] * pos[None, :] % total
    angle = phase.astype(jnp.float32) * (2.0 * math.pi / total)
    both = jnp.stack([jnp.cos(angle), -jnp.sin(angle)], axis=1)
    factor = (jnp.where(kays == 0, 1.0, 2.0) / total).astype(jnp.float32)[:, None, None]
    forward = both.astype(jnp.bfloat16).reshape(2 * MODES, count)
    inverse = (both * factor).astype(jnp.bfloat16).reshape(2 * MODES, count)
    return forward, inverse


def exchange_kernel(
    nr, nc, layer, x_in, y_in, wx, wy, x_out, y_out, x_got, y_got, x_w, y_w, x_mat, y_mat,
    w_sem, xs_send, xs_recv, ys_send, ys_recv, xg_send, xg_recv, yg_send, yg_recv,
):
    row = lax.axis_index("row")
    col = lax.axis_index("col")

    def row_peer(d):
        return (lax.rem(row + d, nr), col)

    def col_peer(d):
        return (row, lax.rem(col + d, nc))

    y_load = pltpu.make_async_copy(wy.at[layer], y_w, w_sem.at[0])
    x_load = pltpu.make_async_copy(wx.at[layer], x_w, w_sem.at[1])
    y_load.start()
    x_load.start()

    barrier = pltpu.get_barrier_semaphore()
    for d in range(1, nr):
        pl.semaphore_signal(barrier, inc=1, device_id=row_peer(d), device_id_type=MESH)
    for d in range(1, nc):
        pl.semaphore_signal(barrier, inc=1, device_id=col_peer(d), device_id_type=MESH)
    pl.semaphore_wait(barrier, nr + nc - 2)

    def copy(src, dst, send, recv, d, peer):
        made = pltpu.make_async_remote_copy(
            src_ref=src, dst_ref=dst, send_sem=send.at[d], recv_sem=recv.at[d],
            device_id=peer, device_id_type=MESH,
        )
        made.start()
        return made

    x_scatter = [
        copy(x_in.at[row_peer(d)[0]], x_got.at[d], xs_send, xs_recv, d, row_peer(d))
        for d in range(1, nr)
    ]
    y_scatter = [
        copy(y_in.at[col_peer(d)[1]], y_got.at[d], ys_send, ys_recv, d, col_peer(d))
        for d in range(1, nc)
    ]

    for load, w, mat in ((y_load, y_w, y_mat), (x_load, x_w, x_mat)):
        load.wait()
        for k in range(MODES):
            real = w[0, k]
            imag = w[1, k]
            top = jnp.concatenate([real, imag], axis=1)
            bottom = jnp.concatenate([-imag, real], axis=1)
            mat[k] = jnp.concatenate([top, bottom], axis=0).astype(jnp.bfloat16)

    def mix(own, first, got, n, mat, out):
        for k in range(MODES):
            total = first[own, k].astype(jnp.float32)
            for d in range(1, n):
                total = total + got[d, k].astype(jnp.float32)
            out[own, k] = jnp.dot(
                total.astype(jnp.bfloat16), mat[k], preferred_element_type=jnp.float32
            ).astype(jnp.bfloat16)

    for made in y_scatter:
        made.wait()
    mix(col, y_in, y_got, nc, y_mat, y_out)
    y_gather = [
        copy(y_out.at[col], y_out.at[col], yg_send, yg_recv, d, col_peer(d))
        for d in range(1, nc)
    ]
    for made in x_scatter:
        made.wait()
    mix(row, x_in, x_got, nr, x_mat, x_out)
    x_gather = [
        copy(x_out.at[row], x_out.at[row], xg_send, xg_recv, d, row_peer(d))
        for d in range(1, nr)
    ]
    for made in y_gather + x_gather:
        made.wait()


def exchange(x_part, y_part, wx, wy, layer):
    nr, nc = lax.axis_size("row"), lax.axis_size("col")
    wide = x_part.shape[-1]
    dma = pltpu.SemaphoreType.DMA
    whole = pl.BlockSpec(memory_space=VMEM)
    return pl.pallas_call(
        functools.partial(exchange_kernel, nr, nc, layer),
        out_shape=(
            jax.ShapeDtypeStruct(x_part.shape, jnp.bfloat16),
            jax.ShapeDtypeStruct(y_part.shape, jnp.bfloat16),
        ),
        in_specs=[whole, whole] + [pl.BlockSpec(memory_space=pl.ANY)] * 2,
        out_specs=(whole, whole),
        scratch_shapes=[
            VMEM(x_part.shape, jnp.bfloat16),
            VMEM(y_part.shape, jnp.bfloat16),
            VMEM(wx.shape[1:], jnp.float32),
            VMEM(wy.shape[1:], jnp.float32),
            VMEM((MODES, wide, wide), jnp.bfloat16),
            VMEM((MODES, wide, wide), jnp.bfloat16),
            dma((2,)),
            dma((nr,)), dma((nr,)), dma((nc,)), dma((nc,)),
            dma((nr,)), dma((nr,)), dma((nc,)), dma((nc,)),
        ],
        compiler_params=pltpu.CompilerParams(
            collective_id=layer, has_side_effects=True, vmem_limit_bytes=32 << 20
        ),
        name="exchange",
    )(x_part, y_part, wx, wy)


def dot(a, b, contract=((1,), (0,))):
    return lax.dot_general(a, b, (contract, ((), ())), preferred_element_type=jnp.float32)


def y_modes(line, state, fyc, fys, y_rows, lines):
    both = ((1,), (1,))
    parts = jnp.concatenate([dot(fyc, state, both), dot(fys, state, both)], axis=1)
    y_rows[pl.ds(line, MODES, stride=lines), :] = parts


def put_parts(x_rows, y_rows, x_part, y_part):
    nr, _, x_own, wide = x_part.shape
    nc, _, y_own, _ = y_part.shape
    for k in range(MODES):
        turned = x_rows[k * wide:(k + 1) * wide, :].T
        for i in range(nr):
            x_part[i, k] = turned[i * x_own:(i + 1) * x_own].astype(jnp.bfloat16)
        for i in range(nc):
            at = k * nc * y_own + i * y_own
            y_part[i, k] = y_rows[at:at + y_own, :].astype(jnp.bfloat16)


def start_kernel(field, fx, fyc, fys, state, x_part, y_part, big, x_rows, y_rows):
    channels, lines, _ = field.shape
    for c in range(channels):
        plane = field[c]
        x_rows[pl.ds(c, 2 * MODES, stride=channels), :] = dot(fx[...], plane)
        big[pl.ds(c, lines, stride=channels), :] = plane.astype(jnp.float32)

    def body(x, carry):
        here = big[pl.ds(pl.multiple_of(x * channels, channels), channels), :].astype(jnp.bfloat16)
        state[x] = here
        y_modes(x, here, fyc[...], fys[...], y_rows, lines)
        return carry

    lax.fori_loop(0, lines, body, 0, unroll=4)
    put_parts(x_rows, y_rows, x_part, y_part)


def layer_kernel(last, state, x_mixed, y_mixed, gx, gyc, gys, up, bias, down, *rest):
    if last:
        out, big, x_rows, y_rows, flat = rest
    else:
        fx, fyc, fys, out, x_part, y_part, big, x_rows, y_rows, flat = rest
    lines, channels, cols = state.shape
    both = 2 * MODES
    nr, _, x_own, _ = x_mixed.shape
    nc, _, y_own, _ = y_mixed.shape
    for k in range(MODES):
        for i in range(nr):
            flat[k, i * x_own:(i + 1) * x_own, :] = x_mixed[i, k].astype(jnp.float32)
        for i in range(nc):
            at = k * lines + i * y_own
            y_rows[at:at + y_own, :] = y_mixed[i, k].astype(jnp.float32)
    for k in range(MODES):
        turned = flat[k].T
        for part in range(2):
            x_rows[pl.ds(2 * k + part, channels, stride=both), :] = turned[
                part * channels:(part + 1) * channels
            ]
    for o in range(channels):
        modes = x_rows[o * both:(o + 1) * both, :].astype(jnp.bfloat16)
        big[pl.ds(o, lines, stride=channels), :] = dot(gx[...], modes)

    def body(x, carry):
        here = pl.ds(pl.multiple_of(x * channels, channels), channels)
        turned = y_rows[pl.ds(x, MODES, stride=lines), :].T.astype(jnp.bfloat16)
        back_y = dot(turned[:channels], gyc[...]) + dot(turned[channels:], gys[...])
        gline = (state[x].astype(jnp.float32) + big[here, :] + back_y).astype(jnp.bfloat16)
        hidden = dot(up[...], gline) + bias[...]
        hidden = (0.5 * hidden * (1.0 + lax.erf(hidden * math.sqrt(0.5)))).astype(jnp.bfloat16)
        fresh = gline.astype(jnp.float32) + dot(down[...], hidden)
        if last:
            big[here, :] = fresh
        else:
            rounded = fresh.astype(jnp.bfloat16)
            big[here, :] = rounded.astype(jnp.float32)
            out[x] = rounded
            y_modes(x, rounded, fyc[...], fys[...], y_rows, lines)
        return carry

    lax.fori_loop(0, lines, body, 0, unroll=2)
    for c in range(channels):
        plane = big[pl.ds(c, lines, stride=channels), :].astype(jnp.bfloat16)
        if last:
            out[c] = plane
        else:
            x_rows[pl.ds(c, both, stride=channels), :] = dot(fx[...], plane)
    if not last:
        put_parts(x_rows, y_rows, x_part, y_part)


def local_call(kernel, name, out_shape, scratch, *args):
    whole = pl.BlockSpec(memory_space=VMEM)
    return pl.pallas_call(
        kernel,
        out_shape=out_shape,
        in_specs=[whole] * len(args),
        out_specs=jax.tree.map(lambda _: whole, out_shape),
        scratch_shapes=[VMEM(shape, jnp.float32) for shape in scratch],
        compiler_params=pltpu.CompilerParams(vmem_limit_bytes=32 << 20),
        name=name,
    )(*args)


def on_device(field, x_weight, y_weight, up_weight, up_bias, down_weight):
    planes, channels, lines, cols = field.shape
    nr, nc = lax.axis_size("row"), lax.axis_size("col")
    fx, gx = tables(lines * nr, lax.axis_index("row") * lines, lines)
    fy, gy = tables(cols * nc, lax.axis_index("col") * cols, cols)
    gx = gx.T
    fyc, fys, gyc, gys = fy[0::2], fy[1::2], gy[0::2], gy[1::2]
    half = jnp.bfloat16
    state_shape = jax.ShapeDtypeStruct((lines, channels, cols), half)
    x_shape = jax.ShapeDtypeStruct((nr, MODES, cols // nr, 2 * channels), half)
    y_shape = jax.ShapeDtypeStruct((nc, MODES, lines // nc, 2 * channels), half)
    scratch = [(lines * channels, cols), (2 * MODES * channels, cols), (MODES * lines, 2 * channels)]
    more = scratch + [(MODES, cols, 2 * channels)]
    results = []
    for z in range(planes):
        state, x_part, y_part = local_call(
            start_kernel, "start", (state_shape, x_shape, y_shape), scratch, field[z], fx, fyc, fys
        )
        for layer in range(LAYERS):
            last = layer == LAYERS - 1
            x_mixed, y_mixed = exchange(x_part, y_part, x_weight, y_weight, layer)
            args = (
                state, x_mixed, y_mixed, gx, gyc, gys,
                up_weight[layer], up_bias[layer][:, None], down_weight[layer],
            )
            kernel = functools.partial(layer_kernel, last)
            if last:
                shape = jax.ShapeDtypeStruct((channels, lines, cols), half)
                results.append(local_call(kernel, "finish", shape, more, *args))
            else:
                state, x_part, y_part = local_call(
                    kernel, "layer", (state_shape, x_shape, y_shape), more, *args, fx, fyc, fys
                )
    return jnp.stack(results)


def solution(mesh):
    in_specs = (P(None, None, "row", "col"), P(), P(), P(), P(), P())
    out_specs = P(None, None, "row", "col")
    return jax.shard_map(
        on_device, mesh=mesh, in_specs=in_specs, out_specs=out_specs, check_vma=False
    )
```

```python
import functools
import math

import jax
import jax.numpy as jnp
from jax import lax
from jax.experimental import pallas as pl
from jax.experimental.pallas import tpu as pltpu
from jax.sharding import PartitionSpec as P

MODES = 12
LAYERS = 2
MESH = pl.DeviceIdType.MESH
VMEM = pltpu.VMEM


def tables(total, start, count):
    pos = start + jnp.arange(count, dtype=jnp.int32)
    kays = jnp.arange(MODES, dtype=jnp.int32)
    phase = kays[:, None] * pos[None, :] % total
    angle = phase.astype(jnp.float32) * (2.0 * math.pi / total)
    both = jnp.stack([jnp.cos(angle), -jnp.sin(angle)], axis=1)
    factor = (jnp.where(kays == 0, 1.0, 2.0) / total).astype(jnp.float32)[:, None, None]
    forward = both.astype(jnp.bfloat16).reshape(2 * MODES, count)
    inverse = (both * factor).astype(jnp.bfloat16).reshape(2 * MODES, count)
    return forward, inverse


def dot(a, b, contract=((1,), (0,))):
    return lax.dot_general(a, b, (contract, ((), ())), preferred_element_type=jnp.float32)


def whole_kernel(
    nr, nc, field_in, fx_ref, gx_ref, fy_ref, gy_ref, wx, wy, up_in, bias_in, down_in, out,
    field, up_ref, bias_ref, down_ref, state, x_part, y_part, x_got, y_got, x_all, y_all, x_w, y_w, x_mat, y_mat,
    big, base, x_rows, y_rows, flat,
    w_sem, xs_send, xs_recv, ys_send, ys_recv, xg_send, xg_recv, yg_send, yg_recv,
):
    row = lax.axis_index("row")
    col = lax.axis_index("col")
    channels, lines, cols = field.shape
    both = 2 * MODES
    wide = 2 * channels
    x_own, y_own = cols // nr, lines // nc
    group = math.gcd(lines, 4)

    def row_peer(d):
        return (lax.rem(row + d, nr), col)

    def col_peer(d):
        return (row, lax.rem(col + d, nc))

    loads = [
        pltpu.make_async_copy(src, dst, w_sem.at[i])
        for i, (src, dst) in enumerate((
            (field_in, field), (wy, y_w), (wx, x_w), (up_in, up_ref), (bias_in, bias_ref),
            (down_in, down_ref),
        ))
    ]
    for load in loads:
        load.start()

    barrier = pltpu.get_barrier_semaphore()
    for d in range(1, nr):
        pl.semaphore_signal(barrier, inc=1, device_id=row_peer(d), device_id_type=MESH)
    for d in range(1, nc):
        pl.semaphore_signal(barrier, inc=1, device_id=col_peer(d), device_id_type=MESH)

    def copy(src, dst, send, recv, peer):
        made = pltpu.make_async_remote_copy(
            src_ref=src, dst_ref=dst, send_sem=send, recv_sem=recv,
            device_id=peer, device_id_type=MESH,
        )
        made.start()
        return made

    def stacked(x):
        return pl.ds(pl.multiple_of(x * channels, channels), channels)

    def mix(own, first, got, n, mat, result):
        for k in range(MODES):
            total = first[own, k].astype(jnp.float32)
            for d in range(1, n):
                total = total + got[d, k].astype(jnp.float32)
            result[own, k] = dot(total.astype(jnp.bfloat16), mat[k]).astype(jnp.bfloat16)

    loads[0].wait()
    for c in range(channels):
        big[pl.ds(c, lines, stride=channels), :] = field[c].astype(jnp.float32)

    for layer in range(LAYERS):
        for c in range(channels):
            if layer == 0:
                plane = field[c]
            else:
                plane = big[pl.ds(c, lines, stride=channels), :].astype(jnp.bfloat16)
            x_rows[pl.ds(c, both, stride=channels), :] = dot(fx_ref[...], plane)
        for k in range(MODES):
            turned = x_rows[k * wide:(k + 1) * wide, :].T
            for i in range(nr):
                x_part[i, k] = turned[i * x_own:(i + 1) * x_own].astype(jnp.bfloat16)
        if layer == 0:
            pl.semaphore_wait(barrier, nr + nc - 2)
        x_scatter = [
            copy(x_part.at[row_peer(d)[0]], x_got.at[layer, d], xs_send.at[layer, d],
                 xs_recv.at[layer, d], row_peer(d))
            for d in range(1, nr)
        ]

        def forward_y(step, carry):
            at = step * group
            many = []
            for j in range(group):
                fresh = big[stacked(at + j), :].astype(jnp.bfloat16)
                if layer == 0:
                    state[at + j] = fresh
                many.append(fresh)
            parts = dot(fy_ref[...], jnp.concatenate(many, axis=0), ((1,), (1,)))
            for j in range(group):
                here = slice(j * channels, (j + 1) * channels)
                y_rows[pl.ds(at + j, MODES, stride=lines), :] = jnp.concatenate(
                    [parts[:MODES, here], parts[16:16 + MODES, here]], axis=1
                )
            return carry

        lax.fori_loop(0, lines // group, forward_y, 0, unroll=4)
        for k in range(MODES):
            for i in range(nc):
                at = k * lines + i * y_own
                y_part[i, k] = y_rows[at:at + y_own, :].astype(jnp.bfloat16)
        y_scatter = [
            copy(y_part.at[col_peer(d)[1]], y_got.at[layer, d], ys_send.at[layer, d],
                 ys_recv.at[layer, d], col_peer(d))
            for d in range(1, nc)
        ]

        if layer == 0:
            for load in loads[1:]:
                load.wait()
        for w, mat in ((y_w, y_mat), (x_w, x_mat)):
            for k in range(MODES):
                real = w[layer, 0, k]
                imag = w[layer, 1, k]
                top = jnp.concatenate([real, imag], axis=1)
                bottom = jnp.concatenate([-imag, real], axis=1)
                mat[k] = jnp.concatenate([top, bottom], axis=0).astype(jnp.bfloat16)

        for made in y_scatter:
            made.wait()
        mix(col, y_part, y_got.at[layer], nc, y_mat, y_all.at[layer])
        y_gather = [
            copy(y_all.at[layer, col], y_all.at[layer, col], yg_send.at[layer, d],
                 yg_recv.at[layer, d], col_peer(d))
            for d in range(1, nc)
        ]
        for made in x_scatter:
            made.wait()
        mix(row, x_part, x_got.at[layer], nr, x_mat, x_all.at[layer])
        x_gather = [
            copy(x_all.at[layer, row], x_all.at[layer, row], xg_send.at[layer, d],
                 xg_recv.at[layer, d], row_peer(d))
            for d in range(1, nr)
        ]

        for made in y_gather:
            made.wait()
        for k in range(MODES):
            for i in range(nc):
                at = k * lines + i * y_own
                y_rows[at:at + y_own, :] = y_all[layer, i, k].astype(jnp.float32)

        def inverse_y(step, carry):
            at = step * group
            many = [
                y_rows[pl.ds(at + j, MODES, stride=lines), :].T.astype(jnp.bfloat16)
                for j in range(group)
            ]
            even = jnp.concatenate([one[:channels] for one in many], axis=0)
            odd = jnp.concatenate([one[channels:] for one in many], axis=0)
            back = dot(even, gy_ref[:MODES, :]) + dot(odd, gy_ref[16:16 + MODES, :])
            for j in range(group):
                line = back[j * channels:(j + 1) * channels]
                base[stacked(at + j), :] = state[at + j].astype(jnp.float32) + line
            return carry

        lax.fori_loop(0, lines // group, inverse_y, 0, unroll=4)

        for made in x_gather:
            made.wait()
        for k in range(MODES):
            for i in range(nr):
                flat[k, i * x_own:(i + 1) * x_own, :] = x_all[layer, i, k].astype(jnp.float32)
        for k in range(MODES):
            turned = flat[k].T
            for part in range(2):
                x_rows[pl.ds(2 * k + part, channels, stride=both), :] = turned[
                    part * channels:(part + 1) * channels
                ]
        for o in range(channels):
            modes = x_rows[o * both:(o + 1) * both, :].astype(jnp.bfloat16)
            big[pl.ds(o, lines, stride=channels), :] = dot(gx_ref[...], modes)

        bias = jnp.broadcast_to(bias_ref[layer:layer + 1, :], (8, bias_ref.shape[1])).T[:, :1]

        def feed(step, carry):
            at = step * group
            done = []
            for j in range(group):
                gline = (base[stacked(at + j), :] + big[stacked(at + j), :]).astype(jnp.bfloat16)
                hidden = dot(up_ref[layer], gline) + bias
                hidden = 0.5 * hidden * (1.0 + lax.erf(hidden * math.sqrt(0.5)))
                fresh = gline.astype(jnp.float32) + dot(
                    down_ref[layer], hidden.astype(jnp.bfloat16)
                )
                done.append(fresh.astype(jnp.bfloat16))
            for j in range(group):
                big[stacked(at + j), :] = done[j].astype(jnp.float32)
                if layer < LAYERS - 1:
                    state[at + j] = done[j]
            return carry

        lax.fori_loop(0, lines // group, feed, 0)

    for c in range(channels):
        out[c] = big[pl.ds(c, lines, stride=channels), :].astype(jnp.bfloat16)


def padded(table):
    even, odd = table[0::2], table[1::2]
    gap = ((0, 16 - MODES), (0, 0))
    return jnp.concatenate([jnp.pad(even, gap), jnp.pad(odd, gap)], axis=0)


def on_device(field, x_weight, y_weight, up_weight, up_bias, down_weight):
    planes, channels, lines, cols = field.shape
    nr, nc = lax.axis_size("row"), lax.axis_size("col")
    fx, gx = tables(lines * nr, lax.axis_index("row") * lines, lines)
    fy, gy = tables(cols * nc, lax.axis_index("col") * cols, cols)
    half, full = jnp.bfloat16, jnp.float32
    wide = 2 * channels
    x_shape = (nr, MODES, cols // nr, wide)
    y_shape = (nc, MODES, lines // nc, wide)
    dma = pltpu.SemaphoreType.DMA
    inside = pl.BlockSpec(memory_space=VMEM)
    outside = pl.BlockSpec(memory_space=pltpu.HBM)
    call = pl.pallas_call(
        functools.partial(whole_kernel, nr, nc),
        out_shape=jax.ShapeDtypeStruct((channels, lines, cols), half),
        in_specs=[outside] + [inside] * 4 + [outside] * 5,
        out_specs=inside,
        scratch_shapes=[
            VMEM((channels, lines, cols), half),
            VMEM(up_weight.shape, half),
            VMEM(up_bias.shape, full),
            VMEM(down_weight.shape, half),
            VMEM((lines, channels, cols), half),
            VMEM(x_shape, half),
            VMEM(y_shape, half),
            VMEM((LAYERS,) + x_shape, half),
            VMEM((LAYERS,) + y_shape, half),
            VMEM((LAYERS,) + x_shape, half),
            VMEM((LAYERS,) + y_shape, half),
            VMEM(x_weight.shape, full),
            VMEM(y_weight.shape, full),
            VMEM((MODES, wide, wide), half),
            VMEM((MODES, wide, wide), half),
            VMEM((lines * channels, cols), full),
            VMEM((lines * channels, cols), full),
            VMEM((2 * MODES * channels, cols), full),
            VMEM((MODES * lines, wide), full),
            VMEM((MODES, cols, wide), full),
            dma((6,)),
        ] + [dma((LAYERS, n)) for n in (nr, nr, nc, nc, nr, nr, nc, nc)],
        compiler_params=pltpu.CompilerParams(
            collective_id=0, has_side_effects=True, vmem_limit_bytes=48 << 20
        ),
        name="operator",
    )
    return jnp.stack([
        call(field[z], fx, gx.T, padded(fy), padded(gy), x_weight, y_weight,
             up_weight, up_bias, down_weight)
        for z in range(planes)
    ])


def solution(mesh):
    in_specs = (P(None, None, "row", "col"), P(), P(), P(), P(), P())
    out_specs = P(None, None, "row", "col")
    return jax.shard_map(
        on_device, mesh=mesh, in_specs=in_specs, out_specs=out_specs, check_vma=False
    )
```

```python
import functools
import math

import jax
import jax.numpy as jnp
from jax import lax
from jax.experimental import pallas as pl
from jax.experimental.pallas import tpu as pltpu
from jax.sharding import PartitionSpec as P

MODES = 12
LAYERS = 2
MESH = pl.DeviceIdType.MESH
VMEM = pltpu.VMEM


def tables(total, start, count):
    pos = start + jnp.arange(count, dtype=jnp.int32)
    kays = jnp.arange(MODES, dtype=jnp.int32)
    phase = kays[:, None] * pos[None, :] % total
    angle = phase.astype(jnp.float32) * (2.0 * math.pi / total)
    both = jnp.stack([jnp.cos(angle), -jnp.sin(angle)], axis=1)
    factor = (jnp.where(kays == 0, 1.0, 2.0) / total).astype(jnp.float32)[:, None, None]
    forward = both.astype(jnp.bfloat16).reshape(2 * MODES, count)
    inverse = (both * factor).astype(jnp.bfloat16).reshape(2 * MODES, count)
    return forward, inverse


def dot(a, b, contract=((1,), (0,))):
    return lax.dot_general(a, b, (contract, ((), ())), preferred_element_type=jnp.float32)


def whole_kernel(
    nr, nc, field_in, fx_ref, gx_ref, fy_ref, gy_ref, wx, wy, up_in, bias_in, down_in, out,
    field, up_ref, bias_ref, down_ref, state, x_part, y_part, x_got, y_got, x_all, y_all, x_w, y_w, x_mat, y_mat,
    big, base, x_rows, y_rows, flat,
    w_sem, xs_send, xs_recv, ys_send, ys_recv, xg_send, xg_recv, yg_send, yg_recv,
):
    row = lax.axis_index("row")
    col = lax.axis_index("col")
    channels, lines, cols = field.shape
    both = 2 * MODES
    wide = 2 * channels
    x_own, y_own = cols // nr, lines // nc
    group = math.gcd(lines, 4)

    def row_peer(d):
        return (lax.rem(row + d, nr), col)

    def col_peer(d):
        return (row, lax.rem(col + d, nc))

    loads = [
        pltpu.make_async_copy(src, dst, w_sem.at[i])
        for i, (src, dst) in enumerate((
            (field_in, field), (wy, y_w), (wx, x_w), (up_in, up_ref), (bias_in, bias_ref),
            (down_in, down_ref),
        ))
    ]
    for load in loads:
        load.start()

    barrier = pltpu.get_barrier_semaphore()
    for d in range(1, nr):
        pl.semaphore_signal(barrier, inc=1, device_id=row_peer(d), device_id_type=MESH)
    for d in range(1, nc):
        pl.semaphore_signal(barrier, inc=1, device_id=col_peer(d), device_id_type=MESH)

    def copy(src, dst, send, recv, peer):
        made = pltpu.make_async_remote_copy(
            src_ref=src, dst_ref=dst, send_sem=send, recv_sem=recv,
            device_id=peer, device_id_type=MESH,
        )
        made.start()
        return made

    def stacked(x):
        return pl.ds(pl.multiple_of(x * channels, channels), channels)

    def mix(own, first, got, n, mat, result):
        for k in range(MODES):
            total = first[own, k].astype(jnp.float32)
            for d in range(1, n):
                total = total + got[d, k].astype(jnp.float32)
            result[own, k] = dot(total.astype(jnp.bfloat16), mat[k]).astype(jnp.bfloat16)

    loads[0].wait()
    for c in range(channels):
        big[pl.ds(c, lines, stride=channels), :] = field[c].astype(jnp.float32)

    for layer in range(LAYERS):
        for c in range(channels):
            if layer == 0:
                plane = field[c]
            else:
                plane = big[pl.ds(c, lines, stride=channels), :].astype(jnp.bfloat16)
            x_rows[pl.ds(c, both, stride=channels), :] = dot(fx_ref[...], plane)
        for k in range(MODES):
            turned = x_rows[k * wide:(k + 1) * wide, :].T
            for i in range(nr):
                x_part[i, k] = turned[i * x_own:(i + 1) * x_own].astype(jnp.bfloat16)
        if layer == 0:
            pl.semaphore_wait(barrier, nr + nc - 2)
        x_scatter = [
            copy(x_part.at[row_peer(d)[0]], x_got.at[layer, d], xs_send.at[layer, d],
                 xs_recv.at[layer, d], row_peer(d))
            for d in range(1, nr)
        ]

        def forward_y(step, carry):
            at = step * group
            many = []
            for j in range(group):
                fresh = big[stacked(at + j), :].astype(jnp.bfloat16)
                if layer == 0:
                    state[at + j] = fresh
                many.append(fresh)
            parts = dot(fy_ref[...], jnp.concatenate(many, axis=0), ((1,), (1,)))
            for j in range(group):
                here = slice(j * channels, (j + 1) * channels)
                y_rows[pl.ds(at + j, MODES, stride=lines), :] = jnp.concatenate(
                    [parts[:MODES, here], parts[16:16 + MODES, here]], axis=1
                )
            return carry

        lax.fori_loop(0, lines // group, forward_y, 0, unroll=4)
        for k in range(MODES):
            for i in range(nc):
                at = k * lines + i * y_own
                y_part[i, k] = y_rows[at:at + y_own, :].astype(jnp.bfloat16)
        y_scatter = [
            copy(y_part.at[col_peer(d)[1]], y_got.at[layer, d], ys_send.at[layer, d],
                 ys_recv.at[layer, d], col_peer(d))
            for d in range(1, nc)
        ]

        if layer == 0:
            for load in loads[1:]:
                load.wait()
        for w, mat in ((y_w, y_mat), (x_w, x_mat)):
            for k in range(MODES):
                real = w[layer, 0, k]
                imag = w[layer, 1, k]
                top = jnp.concatenate([real, imag], axis=1)
                bottom = jnp.concatenate([-imag, real], axis=1)
                mat[k] = jnp.concatenate([top, bottom], axis=0).astype(jnp.bfloat16)

        for made in y_scatter:
            made.wait()
        mix(col, y_part, y_got.at[layer], nc, y_mat, y_all.at[layer])
        y_gather = [
            copy(y_all.at[layer, col], y_all.at[layer, col], yg_send.at[layer, d],
                 yg_recv.at[layer, d], col_peer(d))
            for d in range(1, nc)
        ]
        for made in x_scatter:
            made.wait()
        mix(row, x_part, x_got.at[layer], nr, x_mat, x_all.at[layer])
        x_gather = [
            copy(x_all.at[layer, row], x_all.at[layer, row], xg_send.at[layer, d],
                 xg_recv.at[layer, d], row_peer(d))
            for d in range(1, nr)
        ]

        for made in y_gather:
            made.wait()
        for k in range(MODES):
            for i in range(nc):
                at = k * lines + i * y_own
                y_rows[at:at + y_own, :] = y_all[layer, i, k].astype(jnp.float32)

        def inverse_y(step, carry):
            at = step * group
            many = [
                y_rows[pl.ds(at + j, MODES, stride=lines), :].T.astype(jnp.bfloat16)
                for j in range(group)
            ]
            even = jnp.concatenate([one[:channels] for one in many], axis=0)
            odd = jnp.concatenate([one[channels:] for one in many], axis=0)
            back = dot(even, gy_ref[:MODES, :]) + dot(odd, gy_ref[16:16 + MODES, :])
            for j in range(group):
                line = back[j * channels:(j + 1) * channels]
                base[stacked(at + j), :] = state[at + j].astype(jnp.float32) + line
            return carry

        lax.fori_loop(0, lines // group, inverse_y, 0, unroll=4)

        for made in x_gather:
            made.wait()
        for k in range(MODES):
            for i in range(nr):
                flat[k, i * x_own:(i + 1) * x_own, :] = x_all[layer, i, k].astype(jnp.float32)
        for k in range(MODES):
            turned = flat[k].T
            for part in range(2):
                x_rows[pl.ds(2 * k + part, channels, stride=both), :] = turned[
                    part * channels:(part + 1) * channels
                ]
        for o in range(channels):
            modes = x_rows[o * both:(o + 1) * both, :].astype(jnp.bfloat16)
            big[pl.ds(o, lines, stride=channels), :] = dot(gx_ref[...], modes)

        bias = jnp.broadcast_to(bias_ref[layer:layer + 1, :], (8, bias_ref.shape[1])).T[:, :1]

        def feed(step, carry):
            at = step * group
            done = []
            for j in range(group):
                gline = (base[stacked(at + j), :] + big[stacked(at + j), :]).astype(jnp.bfloat16)
                hidden = dot(up_ref[layer], gline) + bias
                hidden = hidden * (1.0 + lax.erf(hidden * math.sqrt(0.5)))
                fresh = gline.astype(jnp.float32) + 0.5 * dot(
                    down_ref[layer], hidden.astype(jnp.bfloat16)
                )
                done.append(fresh.astype(jnp.bfloat16))
            for j in range(group):
                big[stacked(at + j), :] = done[j].astype(jnp.float32)
                if layer < LAYERS - 1:
                    state[at + j] = done[j]
            return carry

        lax.fori_loop(0, lines // group, feed, 0)

    for c in range(channels):
        out[c] = big[pl.ds(c, lines, stride=channels), :].astype(jnp.bfloat16)


def padded(table):
    even, odd = table[0::2], table[1::2]
    gap = ((0, 16 - MODES), (0, 0))
    return jnp.concatenate([jnp.pad(even, gap), jnp.pad(odd, gap)], axis=0)


def on_device(field, x_weight, y_weight, up_weight, up_bias, down_weight):
    planes, channels, lines, cols = field.shape
    nr, nc = lax.axis_size("row"), lax.axis_size("col")
    fx, gx = tables(lines * nr, lax.axis_index("row") * lines, lines)
    fy, gy = tables(cols * nc, lax.axis_index("col") * cols, cols)
    half, full = jnp.bfloat16, jnp.float32
    wide = 2 * channels
    x_shape = (nr, MODES, cols // nr, wide)
    y_shape = (nc, MODES, lines // nc, wide)
    dma = pltpu.SemaphoreType.DMA
    inside = pl.BlockSpec(memory_space=VMEM)
    outside = pl.BlockSpec(memory_space=pltpu.HBM)
    call = pl.pallas_call(
        functools.partial(whole_kernel, nr, nc),
        out_shape=jax.ShapeDtypeStruct((channels, lines, cols), half),
        in_specs=[outside] + [inside] * 4 + [outside] * 5,
        out_specs=inside,
        scratch_shapes=[
            VMEM((channels, lines, cols), half),
            VMEM(up_weight.shape, half),
            VMEM(up_bias.shape, full),
            VMEM(down_weight.shape, half),
            VMEM((lines, channels, cols), half),
            VMEM(x_shape, half),
            VMEM(y_shape, half),
            VMEM((LAYERS,) + x_shape, half),
            VMEM((LAYERS,) + y_shape, half),
            VMEM((LAYERS,) + x_shape, half),
            VMEM((LAYERS,) + y_shape, half),
            VMEM(x_weight.shape, full),
            VMEM(y_weight.shape, full),
            VMEM((MODES, wide, wide), half),
            VMEM((MODES, wide, wide), half),
            VMEM((lines * channels, cols), full),
            VMEM((lines * channels, cols), full),
            VMEM((2 * MODES * channels, cols), full),
            VMEM((MODES * lines, wide), full),
            VMEM((MODES, cols, wide), full),
            dma((6,)),
        ] + [dma((LAYERS, n)) for n in (nr, nr, nc, nc, nr, nr, nc, nc)],
        compiler_params=pltpu.CompilerParams(
            collective_id=0, has_side_effects=True, vmem_limit_bytes=65000 << 10
        ),
        name="operator",
    )
    return jnp.stack([
        call(field[z], fx, gx.T, padded(fy), padded(gy), x_weight, y_weight,
             up_weight, up_bias, down_weight)
        for z in range(planes)
    ])


def solution(mesh):
    in_specs = (P(None, None, "row", "col"), P(), P(), P(), P(), P())
    out_specs = P(None, None, "row", "col")
    return jax.shard_map(
        on_device, mesh=mesh, in_specs=in_specs, out_specs=out_specs, check_vma=False
    )
```
